32 devices in a mesh: replica: 4 (over y, core), shard: 8 (over z, x).
Axes of the slice: x: 2, y: 2, z: 4, core: 2. Of those that a mesh axis runs over, the one named last changes fastest.
Arguments:
- tokens: bfloat16 [4, 1024, 3072], P('replica', 'shard'), may hold values from -6 to 6
- weight_slots: bfloat16 [4, 576, 128, 128], P('replica', 'shard'), may hold values from -0.15625 to 0.15625
- block_rows: int32 [96, 12], replicated, may hold values from 0 to 23, as said below
- block_owner: int32 [96, 12], replicated, may hold values from 0 to 7, as said below
- block_slot: int32 [96, 12], replicated, may hold values from 0 to 71, as said below
- grad_act: bfloat16 [4, 1024, 12288], P(None, 'shard', 'replica'), may hold values from -6 to 6
Outputs:
- act_out: bfloat16 [4, 1024, 12288], P(None, 'shard', 'replica')
- grad_tokens: bfloat16 [4, 1024, 3072], P('replica', 'shard')
- grad_slots: float32 [4, 576, 128, 128], P('replica', 'shard')
The draws below stay inside these ranges and needn't reach their ends.
Inputs may be any that keep to these rules, and one draw needn't show every extreme that they name: `block_rows`: each row holds 12 distinct increasing block rows; within each group of 24 consecutive block columns every block row appears in exactly 12 of them. `block_owner`: within each group of 24 consecutive block columns no owner holds more than 72 blocks, and in every group some owner holds exactly 72. `block_slot`: within each group of 24 consecutive block columns the pairs of owner and slot are distinct.
All inputs are finite; a program needn't handle non-finite values.
Results may differ from the reference program's by a relative error of at most 0.01.
Values may be sent and summed in bfloat16 or wider, within the bound.
A program may use at most 192 MiB of HBM per device.

```python
import math
import jax
import jax.numpy as jnp
from jax import lax

D = 3072
FF = 12288
BLOCK = 128
TOK_DEV = 128
ROWS = 1024
RB = 24
KEEP = 12
COLS = 96
SLICE_COLS = 24
CAP = 72
N_REPLICA = 4
N_SHARD = 8


def pattern_rows(key):

    def one_slice(slice_key):
        row_key, col_key = jax.random.split(slice_key)
        row_pos = jnp.argsort(jax.random.permutation(row_key, RB))
        col_pos = jnp.argsort(jax.random.permutation(col_key, SLICE_COLS))
        offset = (row_pos[None, :] - 2 * col_pos[:, None]) % RB
        kept = (offset < KEEP).astype(jnp.int32)
        score = (1 - kept) * RB + jnp.arange(RB, dtype=jnp.int32)[None, :]
        return jnp.argsort(score, axis=1)[:, :KEEP].astype(jnp.int32)
    slice_keys = jax.random.split(jax.random.fold_in(key, 7), N_REPLICA)
    return jax.vmap(one_slice)(slice_keys).reshape(COLS, KEEP)


def owner_layout(key):

    def one_slice(slice_key):
        full_key, order_key, shuffle_key = jax.random.split(slice_key, 3)
        full_owner = jax.random.randint(full_key, (), 0, N_SHARD)
        spots = jnp.arange(N_SHARD * CAP, dtype=jnp.int32)
        order = jax.random.permutation(order_key, N_SHARD * CAP).astype(jnp.int32)
        score = order + (spots // CAP != full_owner).astype(jnp.int32) * (N_SHARD * CAP)
        chosen = jnp.argsort(score)[:SLICE_COLS * KEEP]
        chosen = chosen[jax.random.permutation(shuffle_key, SLICE_COLS * KEEP)]
        return chosen.reshape(SLICE_COLS, KEEP)
    slice_keys = jax.random.split(jax.random.fold_in(key, 13), N_REPLICA)
    return jax.vmap(one_slice)(slice_keys).reshape(COLS, KEEP).astype(jnp.int32)


def draw_block_rows(key, part):
    return pattern_rows(key)


def draw_block_owner(key, part):
    return owner_layout(key) // CAP


def draw_block_slot(key, part):
    return owner_layout(key) % CAP


def block_levels(key, extent, shards, smallest, largest):
    level, own = 1.0, jax.random.fold_in(key, 6)
    for position, blocks in shards:
        draws = jnp.exp(jax.random.uniform(jax.random.fold_in(own, position), (blocks,), jnp.float32, smallest / len(shards), largest / len(shards)))
        level = level * jnp.repeat(draws, extent[position] // blocks).reshape([-1 if axis == position else 1 for axis in range(len(extent))])
    return level


def centred(rng, extent, scale, most, cuts=(), kind=jnp.bfloat16):
    entries = scale * jax.random.normal(rng, extent, jnp.float32)
    if cuts:
        entries = entries * block_levels(rng, extent, cuts, -0.22, 0.18)
    return jnp.clip(entries, -most, most).astype(kind)


def setup_inputs(seed: int = 0) -> dict:
    splits = jax.random.split(jax.random.key(seed), 7)
    return {
        "tokens": centred(splits[0], (N_REPLICA, ROWS, D), 1.0, 6.0, ((0, 4), (1, 8))),
        "weight_slots": centred(splits[1], (N_REPLICA, N_SHARD * CAP, BLOCK, BLOCK), (D // 2) ** -0.5, 0.15625, ((0, 4), (1, 8))),
        "block_rows": draw_block_rows(jax.random.fold_in(splits[6], 71), 0),
        "block_owner": draw_block_owner(jax.random.fold_in(splits[6], 71), 0),
        "block_slot": draw_block_slot(jax.random.fold_in(splits[6], 71), 0),
        "grad_act": centred(splits[5], (N_REPLICA, ROWS, FF), 1.0, 6.0, ((1, 8), (2, 4))),
    }


def gelu_value(hidden):
    return 0.5 * hidden * (1.0 + lax.erf(hidden * 0.7071067811865476))

def gelu_slope(hidden):
    normal_cdf = 0.5 * (1.0 + lax.erf(hidden * 0.7071067811865476))
    return normal_cdf + hidden * jnp.exp(-0.5 * hidden * hidden) * 0.3989422804014327

def reference(tokens, weight_slots, block_rows, block_owner, block_slot, grad_act):
    per_group = tokens.reshape(N_REPLICA, N_SHARD, TOK_DEV, RB, BLOCK)
    slot_sets = weight_slots.reshape(N_REPLICA, N_SHARD * CAP, BLOCK, BLOCK)
    rows_all = block_rows.reshape(N_REPLICA, SLICE_COLS, KEEP)
    place_all = (block_owner * CAP + block_slot).reshape(N_REPLICA, SLICE_COLS, KEEP)
    cot_all = grad_act.reshape(N_REPLICA, N_SHARD, TOK_DEV, N_REPLICA, SLICE_COLS, BLOCK)
    cot_slices = jnp.moveaxis(cot_all, (3, 4), (0, 1))
    grad_scale = 1.0 / math.sqrt(N_REPLICA * N_SHARD * TOK_DEV)
    zero_part = jnp.zeros((N_REPLICA, N_SHARD, TOK_DEV, RB, BLOCK), jnp.float32)

    def one_slice(total, inputs):
        rows_q, place_q, slots_q, cot_q = inputs

        def one_column(part, col_in):
            rows_c, place_c, cot_c = col_in
            col_inputs = jnp.take(per_group, rows_c, axis=3).reshape(N_REPLICA, N_SHARD, TOK_DEV, KEEP * BLOCK)
            weight_col = jnp.take(slots_q, place_c, axis=0).reshape(KEEP * BLOCK, BLOCK)
            hidden = jnp.dot(col_inputs, weight_col, preferred_element_type=jnp.float32)
            act_col = gelu_value(hidden).astype(jnp.bfloat16)
            slope = (cot_c.astype(jnp.float32) * gelu_slope(hidden)).astype(jnp.bfloat16)
            terms = jnp.einsum('rstk,rstj->skj', col_inputs.astype(jnp.float32), slope.astype(jnp.float32), precision=lax.Precision.HIGHEST)
            terms = lax.optimization_barrier(terms.astype(jnp.bfloat16)).astype(jnp.float32)
            grad_block = lax.optimization_barrier(jnp.sum(terms, axis=0)).reshape(KEEP, BLOCK, BLOCK)
            grad_in = lax.dot_general(slope, weight_col, (((3,), (1,)), ((), ())), preferred_element_type=jnp.float32)
            part = part.at[:, :, :, rows_c].add(grad_in.reshape(N_REPLICA, N_SHARD, TOK_DEV, KEEP, BLOCK))
            return (part, (act_col, grad_block))
        part, (act_cols, grad_blocks) = lax.scan(one_column, zero_part, (rows_q, place_q, cot_q))
        rounded = lax.optimization_barrier(part.astype(jnp.bfloat16)).astype(jnp.float32)
        slot_grid = jnp.zeros((N_SHARD * CAP, BLOCK, BLOCK), jnp.float32)
        slot_grid = slot_grid.at[place_q.reshape(-1)].set(grad_blocks.reshape(-1, BLOCK, BLOCK))
        return (total + rounded, (act_cols, slot_grid * grad_scale))
    total, (act_all, grids) = lax.scan(one_slice, zero_part, (rows_all, place_all, slot_sets, cot_slices))
    act_out = jnp.transpose(act_all, (2, 3, 4, 0, 1, 5)).reshape(N_REPLICA, ROWS, FF)
    grad_tokens = total.astype(jnp.bfloat16).reshape(N_REPLICA, ROWS, D)
    grad_slots = grids.reshape(N_REPLICA, N_SHARD * CAP, BLOCK, BLOCK)
    return (act_out, grad_tokens, grad_slots)
```

```python
import functools
import math

import jax
import jax.numpy as jnp
from jax import lax
from jax.experimental import pallas as pl
from jax.experimental.pallas import tpu as pltpu
from jax.sharding import PartitionSpec as P

GROUP = 4
PIECES = 6
MIB = 1 << 20


def gelu_both(hidden):
    cdf = 0.5 * (1.0 + lax.erf(hidden * 0.7071067811865476))
    slope = cdf + hidden * jnp.exp(-0.5 * hidden * hidden) * 0.3989422804014327
    return hidden * cdf, slope


def load_columns(step, slot, keep, idx_ref, rows_ref, slab_ref, wbuf, wsem):
    block = slab_ref.shape[1]
    wbuf[slot] = jnp.zeros(wbuf.shape[1:], wbuf.dtype)
    for col in range(GROUP):

        def body(j, carry, col=col):
            at = (step * GROUP + col) * keep + j
            row = pl.multiple_of(rows_ref[at] * block, block)
            pltpu.make_async_copy(
                slab_ref.at[idx_ref[at]],
                wbuf.at[slot, pl.ds(row, block), pl.ds(col * block, block)],
                wsem.at[slot],
            ).start()
            return carry

        lax.fori_loop(0, keep, body, 0)


def wait_columns(slot, keep, block, wbuf, wsem):
    part = wbuf.at[slot, pl.ds(0, keep * block), :]
    pltpu.make_async_copy(part, part, wsem.at[slot]).wait()


def forward_kernel(keep, idx_ref, rows_ref, pos_ref, tok_ref, tokt_ref, cot_ref, slab_ref,
                   act_ref, slope_ref, grads_ref, wbuf, gbuf, wsem, gsem):
    step = pl.program_id(0)
    steps = pl.num_programs(0)
    slot = lax.rem(step, 2)
    block = slab_ref.shape[1]
    rows = tok_ref.shape[0]
    width = tok_ref.shape[1]
    load = functools.partial(load_columns, keep=keep, idx_ref=idx_ref, rows_ref=rows_ref,
                             slab_ref=slab_ref, wbuf=wbuf, wsem=wsem)

    @pl.when(step == 0)
    def _():
        load(step, 0)

    @pl.when(step + 1 < steps)
    def _():
        load(step + 1, 1 - slot)

    wait_columns(slot, keep, block, wbuf, wsem)
    per = cot_ref.shape[1]

    def fwd(r, carry):
        at = pl.ds(pl.multiple_of(r * per, per), per)
        hidden = jnp.dot(tok_ref[at, :], wbuf[slot], preferred_element_type=jnp.float32)
        act, slope = gelu_both(hidden)
        act_ref[r] = act.astype(act_ref.dtype)
        slope = cot_ref[r].astype(jnp.float32) * slope
        slope_ref[at, :] = slope.astype(slope_ref.dtype)
        return carry

    lax.fori_loop(0, cot_ref.shape[0], fwd, 0)

    def drain(which):
        part = gbuf.at[which, pl.ds(0, keep * block), :]
        pltpu.make_async_copy(part, part, gsem.at[which]).wait()

    @pl.when(step >= 2)
    def _():
        drain(slot)

    tile = 512

    def back(m, carry):
        at = pl.ds(pl.multiple_of(m * tile, tile), tile)
        gbuf[slot, at, :] = jnp.dot(
            tokt_ref[at, :], slope_ref[...], preferred_element_type=jnp.float32
        ).astype(gbuf.dtype)
        return carry

    lax.fori_loop(0, width // tile, back, 0)

    for col in range(GROUP):

        def put(j, carry, col=col):
            at = (step * GROUP + col) * keep + j
            row = pl.multiple_of(rows_ref[at] * block, block)
            pltpu.make_async_copy(
                gbuf.at[slot, pl.ds(row, block), pl.ds(col * block, block)],
                grads_ref.at[pos_ref[at]],
                gsem.at[slot],
            ).start()
            return carry

        lax.fori_loop(0, keep, put, 0)

    @pl.when(step == steps - 1)
    def _():
        drain(slot)

        @pl.when(steps > 1)
        def _():
            drain(1 - slot)


def input_grad_kernel(keep, idx_ref, rows_ref, slope_ref, slab_ref, out_ref, wbuf, total, wsem):
    step = pl.program_id(0)
    steps = pl.num_programs(0)
    slot = lax.rem(step, 2)
    block = slab_ref.shape[1]
    load = functools.partial(load_columns, keep=keep, idx_ref=idx_ref, rows_ref=rows_ref,
                             slab_ref=slab_ref, wbuf=wbuf, wsem=wsem)

    @pl.when(step == 0)
    def _():
        load(step, 0)
        total[...] = jnp.zeros_like(total)

    @pl.when(step + 1 < steps)
    def _():
        load(step + 1, 1 - slot)

    wait_columns(slot, keep, block, wbuf, wsem)
    tile = 512

    def body(n, carry):
        at = pl.ds(pl.multiple_of(n * tile, tile), tile)
        total[:, at] += lax.dot_general(
            slope_ref[...], wbuf[slot, at, :], (((1,), (1,)), ((), ())),
            preferred_element_type=jnp.float32,
        )
        return carry

    lax.fori_loop(0, total.shape[1] // tile, body, 0)

    @pl.when(step == steps - 1)
    def _():
        out_ref[...] = total[...].astype(out_ref.dtype)


def gather_blocks(mine, shard_count):
    return lax.all_gather(mine, "shard", axis=0, tiled=False)


def reduce_blocks(grads, shard_count):
    return lax.psum_scatter(grads, "shard", scatter_dimension=0, tiled=False)


def exchange(send):
    return lax.all_to_all(send, "shard", 0, 0, tiled=True)


def local(tokens, weight_slots, block_rows, block_owner, block_slot, grad_act):
    replicas = lax.axis_size("replica")
    shards = lax.axis_size("shard")
    replica = lax.axis_index("replica")
    me = lax.axis_index("shard")
    block = weight_slots.shape[3]
    cap = weight_slots.shape[1]
    tok_rows, width = tokens.shape[1], tokens.shape[2]
    keep = block_rows.shape[1]
    slice_cols = grad_act.shape[2] // block
    all_rows = replicas * tok_rows
    count = slice_cols * keep
    per_pair = -(-cap // shards)
    per_dev = -(-count // (shards * PIECES)) * PIECES
    own_slots = weight_slots.reshape(cap, block, block)

    start_col = replica * slice_cols
    rows = lax.dynamic_slice_in_dim(block_rows, start_col, slice_cols, 0).reshape(-1)
    place = (lax.dynamic_slice_in_dim(block_owner, start_col, slice_cols, 0) * cap
             + lax.dynamic_slice_in_dim(block_slot, start_col, slice_cols, 0)).reshape(-1)
    rank = jnp.sum((place[None, :] < place[:, None]).astype(jnp.int32), axis=1)
    where_at = (rank % shards) * per_dev + rank // shards
    ranks = jnp.arange(count, dtype=jnp.int32)
    by_rank = jnp.sum(jnp.where(rank[None, :] == ranks[:, None], place[None, :], 0), axis=1)
    owners = jnp.arange(shards, dtype=jnp.int32)
    first = jnp.sum((place[None, :] < owners[:, None] * cap).astype(jnp.int32), axis=1)

    turn = jnp.arange(per_pair, dtype=jnp.int32)[None, :]
    my_first = first[me]
    send_rank = my_first + (owners[:, None] - my_first) % shards + turn * shards
    send_slot = jnp.clip(jnp.take(by_rank, jnp.clip(send_rank, 0, count - 1)) - me * cap, 0, cap - 1)
    hold_rank = jnp.clip(jnp.arange(per_dev, dtype=jnp.int32) * shards + me, 0, count - 1)
    hold_owner = jnp.take(by_rank, hold_rank) // cap
    hold_first = jnp.take(first, hold_owner)
    hold_from = hold_owner * per_pair + (hold_rank - hold_first) // shards
    back_rank = first[:, None] + (me - first[:, None]) % shards + turn * shards
    back_from = jnp.clip((back_rank - me) // shards, 0, per_dev - 1)
    slots = me * cap + jnp.arange(cap, dtype=jnp.int32)
    slot_rank = jnp.sum((place[None, :] < slots[:, None]).astype(jnp.int32), axis=1)
    slot_used = jnp.any(place[None, :] == slots[:, None], axis=1)
    slot_from = jnp.clip((slot_rank % shards) * per_pair + (slot_rank - my_first) // shards,
                         0, shards * per_pair - 1)

    gathered = lax.all_gather(tokens, "replica", axis=0, tiled=True).reshape(all_rows, width)
    sent = jnp.take(own_slots, send_slot.reshape(-1), axis=0)
    got = exchange(sent)
    held = jnp.take(got, hold_from, axis=0)
    slab = gather_blocks(held, shards).reshape(shards * per_dev, block, block)
    tok_t = gathered.T

    cols = GROUP * block
    act_out, slope, grads = pl.pallas_call(
        functools.partial(forward_kernel, keep),
        name="forward_and_weight_grad",
        out_shape=(
            jax.ShapeDtypeStruct((replicas, tok_rows, slice_cols * block), jnp.bfloat16),
            jax.ShapeDtypeStruct((all_rows, slice_cols * block), jnp.bfloat16),
            jax.ShapeDtypeStruct((shards * per_dev, block, block), jnp.bfloat16),
        ),
        grid_spec=pltpu.PrefetchScalarGridSpec(
            num_scalar_prefetch=3,
            grid=(slice_cols // GROUP,),
            in_specs=[
                pl.BlockSpec((all_rows, width), lambda i, *_: (0, 0)),
                pl.BlockSpec((width, all_rows), lambda i, *_: (0, 0)),
                pl.BlockSpec((replicas, tok_rows, cols), lambda i, *_: (0, 0, i)),
                pl.BlockSpec(memory_space=pl.ANY),
            ],
            out_specs=(
                pl.BlockSpec((replicas, tok_rows, cols), lambda i, *_: (0, 0, i)),
                pl.BlockSpec((all_rows, cols), lambda i, *_: (0, i)),
                pl.BlockSpec(memory_space=pl.ANY),
            ),
            scratch_shapes=[
                pltpu.VMEM((2, width, cols), jnp.bfloat16),
                pltpu.VMEM((2, width, cols), jnp.bfloat16),
                pltpu.SemaphoreType.DMA((2,)),
                pltpu.SemaphoreType.DMA((2,)),
            ],
        ),
        compiler_params=pltpu.CompilerParams(vmem_limit_bytes=56 * MIB),
        cost_estimate=pl.CostEstimate(
            flops=4 * all_rows * width * slice_cols * block, transcendentals=0,
            bytes_accessed=60 * MIB,
        ),
    )(where_at, rows, where_at, gathered, tok_t, grad_act, slab)

    partial_grad = pl.pallas_call(
        functools.partial(input_grad_kernel, keep),
        name="token_grad",
        out_shape=jax.ShapeDtypeStruct((all_rows, width), jnp.bfloat16),
        grid_spec=pltpu.PrefetchScalarGridSpec(
            num_scalar_prefetch=2,
            grid=(slice_cols // GROUP,),
            in_specs=[
                pl.BlockSpec((all_rows, cols), lambda i, *_: (0, i)),
                pl.BlockSpec(memory_space=pl.ANY),
            ],
            out_specs=pl.BlockSpec((all_rows, width), lambda i, *_: (0, 0)),
            scratch_shapes=[
                pltpu.VMEM((2, width, cols), jnp.bfloat16),
                pltpu.VMEM((all_rows, width), jnp.float32),
                pltpu.SemaphoreType.DMA((2,)),
            ],
        ),
        compiler_params=pltpu.CompilerParams(vmem_limit_bytes=56 * MIB),
        cost_estimate=pl.CostEstimate(
            flops=2 * all_rows * width * slice_cols * block, transcendentals=0,
            bytes_accessed=30 * MIB,
        ),
    )(where_at, rows, slope, slab)

    grad_tokens = lax.psum_scatter(
        partial_grad.reshape(replicas, tok_rows, width), "replica", scatter_dimension=0, tiled=True
    )
    summed = reduce_blocks(grads.reshape(shards, per_dev, block, block), shards)
    summed = summed.reshape(per_dev, block, block)
    returned = exchange(jnp.take(summed, back_from.reshape(-1), axis=0))
    grad_scale = 1.0 / math.sqrt(replicas * shards * tok_rows)
    mine = jnp.take(returned, slot_from, axis=0).astype(jnp.float32) * grad_scale
    grad_slots = jnp.where(slot_used[:, None, None], mine, 0.0).reshape(1, cap, block, block)
    return (act_out, grad_tokens, grad_slots)


def solution(mesh):
    return jax.shard_map(
        local,
        mesh=mesh,
        in_specs=(
            P("replica", "shard", None),
            P("replica", "shard", None, None),
            P(),
            P(),
            P(),
            P(None, "shard", "replica"),
        ),
        out_specs=(
            P(None, "shard", "replica"),
            P("replica", "shard", None),
            P("replica", "shard", None, None),
        ),
        check_vma=False,
    )
```

```python
import functools
import math

import jax
import jax.numpy as jnp
from jax import lax
from jax.experimental import pallas as pl
from jax.experimental.pallas import tpu as pltpu
from jax.sharding import PartitionSpec as P

GROUP = 4
PIECES = 6
CROSS_FIRST = 3
MIB = 1 << 20


def gelu_both(hidden):
    cdf = 0.5 * (1.0 + lax.erf(hidden * 0.7071067811865476))
    slope = cdf + hidden * jnp.exp(-0.5 * hidden * hidden) * 0.3989422804014327
    return hidden * cdf, slope


def load_columns(step, slot, keep, idx_ref, rows_ref, slab_ref, wbuf, wsem):
    block = slab_ref.shape[1]
    wbuf[slot] = jnp.zeros(wbuf.shape[1:], wbuf.dtype)
    for col in range(GROUP):

        def body(j, carry, col=col):
            at = (step * GROUP + col) * keep + j
            row = pl.multiple_of(rows_ref[at] * block, block)
            pltpu.make_async_copy(
                slab_ref.at[idx_ref[at]],
                wbuf.at[slot, pl.ds(row, block), pl.ds(col * block, block)],
                wsem.at[slot],
            ).start()
            return carry

        lax.fori_loop(0, keep, body, 0)


def wait_columns(slot, keep, block, wbuf, wsem):
    part = wbuf.at[slot, pl.ds(0, keep * block), :]
    pltpu.make_async_copy(part, part, wsem.at[slot]).wait()


def forward_kernel(keep, idx_ref, rows_ref, pos_ref, tok_ref, tokt_ref, cot_ref, slab_ref,
                   act_ref, slope_ref, grads_ref, wbuf, gbuf, wsem, gsem):
    step = pl.program_id(0)
    steps = pl.num_programs(0)
    slot = lax.rem(step, 2)
    block = slab_ref.shape[1]
    rows = tok_ref.shape[0]
    width = tok_ref.shape[1]
    load = functools.partial(load_columns, keep=keep, idx_ref=idx_ref, rows_ref=rows_ref,
                             slab_ref=slab_ref, wbuf=wbuf, wsem=wsem)

    @pl.when(step == 0)
    def _():
        load(step, 0)

    @pl.when(step + 1 < steps)
    def _():
        load(step + 1, 1 - slot)

    wait_columns(slot, keep, block, wbuf, wsem)
    per = cot_ref.shape[1]

    def fwd(r, carry):
        at = pl.ds(pl.multiple_of(r * per, per), per)
        hidden = jnp.dot(tok_ref[at, :], wbuf[slot], preferred_element_type=jnp.float32)
        act, slope = gelu_both(hidden)
        act_ref[r] = act.astype(act_ref.dtype)
        slope = cot_ref[r].astype(jnp.float32) * slope
        slope_ref[at, :] = slope.astype(slope_ref.dtype)
        return carry

    lax.fori_loop(0, cot_ref.shape[0], fwd, 0)

    def drain(which):
        part = gbuf.at[which, pl.ds(0, keep * block), :]
        pltpu.make_async_copy(part, part, gsem.at[which]).wait()

    @pl.when(step >= 2)
    def _():
        drain(slot)

    tile = 512

    def back(m, carry):
        at = pl.ds(pl.multiple_of(m * tile, tile), tile)
        gbuf[slot, at, :] = jnp.dot(
            tokt_ref[at, :], slope_ref[...], preferred_element_type=jnp.float32
        ).astype(gbuf.dtype)
        return carry

    lax.fori_loop(0, width // tile, back, 0)

    for col in range(GROUP):

        def put(j, carry, col=col):
            at = (step * GROUP + col) * keep + j
            row = pl.multiple_of(rows_ref[at] * block, block)
            pltpu.make_async_copy(
                gbuf.at[slot, pl.ds(row, block), pl.ds(col * block, block)],
                grads_ref.at[pos_ref[at]],
                gsem.at[slot],
            ).start()
            return carry

        lax.fori_loop(0, keep, put, 0)

    @pl.when(step == steps - 1)
    def _():
        drain(slot)

        @pl.when(steps > 1)
        def _():
            drain(1 - slot)


def input_grad_kernel(keep, idx_ref, rows_ref, slope_ref, slab_ref, out_ref, wbuf, total, wsem):
    step = pl.program_id(0)
    steps = pl.num_programs(0)
    slot = lax.rem(step, 2)
    block = slab_ref.shape[1]
    load = functools.partial(load_columns, keep=keep, idx_ref=idx_ref, rows_ref=rows_ref,
                             slab_ref=slab_ref, wbuf=wbuf, wsem=wsem)

    @pl.when(step == 0)
    def _():
        load(step, 0)
        total[...] = jnp.zeros_like(total)

    @pl.when(step + 1 < steps)
    def _():
        load(step + 1, 1 - slot)

    wait_columns(slot, keep, block, wbuf, wsem)
    tile = 512

    def body(n, carry):
        at = pl.ds(pl.multiple_of(n * tile, tile), tile)
        total[:, at] += lax.dot_general(
            slope_ref[...], wbuf[slot, at, :], (((1,), (1,)), ((), ())),
            preferred_element_type=jnp.float32,
        )
        return carry

    lax.fori_loop(0, total.shape[1] // tile, body, 0)

    @pl.when(step == steps - 1)
    def _():
        out_ref[...] = total[...].astype(out_ref.dtype)


def neighbours(shards):
    me = lax.axis_index("shard")
    return me, me // 2, lax.rem(me, 2), shards // 2


def greet(me, line, length):
    barrier = pltpu.get_barrier_semaphore()
    other = me + 1 - 2 * lax.rem(me, 2)

    def tell(to):
        pl.semaphore_signal(barrier, inc=1, device_id={"shard": to},
                            device_id_type=pl.DeviceIdType.MESH)

    tell(other)

    @pl.when(line < length - 1)
    def _():
        tell(me + 2)

    @pl.when(line > 0)
    def _():
        tell(me - 2)

    pl.semaphore_wait(
        barrier, 1 + (line < length - 1).astype(jnp.int32) + (line > 0).astype(jnp.int32))
    return other


UP, DOWN, ACROSS = 0, 1, 2


def gather_kernel(shards, held_ref, slab_ref, send_sem, recv_sem, own_sem):
    me, line, _, length = neighbours(shards)
    size = held_ref.shape[0] // PIECES
    own = pltpu.make_async_copy(held_ref, slab_ref.at[me], own_sem)
    own.start()
    other = greet(me, line, length)
    targets = (me + 2, me - 2, other)

    def copy(way, source, piece):
        at = pl.ds(piece * size, size)
        return pltpu.make_async_remote_copy(
            src_ref=slab_ref.at[source, at], dst_ref=slab_ref.at[source, at],
            send_sem=send_sem.at[way, source, piece], recv_sem=recv_sem.at[source, piece],
            device_id={"shard": targets[way]}, device_id_type=pl.DeviceIdType.MESH,
        )

    def for_each(first, last, body):
        def step(piece, carry):
            body(piece)
            return carry

        lax.fori_loop(first, last, step, 0)

    def relay(act):
        start, arrive = act

        def own_piece(piece):
            @pl.when(line < length - 1)
            def _():
                start(UP, me, piece)

            @pl.when(line > 0)
            def _():
                start(DOWN, me, piece)

            start(ACROSS, me, piece)

        for_each(0, PIECES, own_piece)
        for far in range(1, length):

            def column(piece, far=far):
                @pl.when(line >= far)
                def _():
                    arrive(me - 2 * far, piece)

                    @pl.when(line < length - 1)
                    def _():
                        start(UP, me - 2 * far, piece)

                    @pl.when(piece >= CROSS_FIRST)
                    def _():
                        start(ACROSS, me - 2 * far, piece)

                @pl.when(line + far < length)
                def _():
                    arrive(me + 2 * far, piece)

                    @pl.when(line > 0)
                    def _():
                        start(DOWN, me + 2 * far, piece)

                    @pl.when(piece >= CROSS_FIRST)
                    def _():
                        start(ACROSS, me + 2 * far, piece)

                if far == 1:
                    arrive(other, piece)

                    @pl.when(piece < CROSS_FIRST)
                    def _():
                        @pl.when(line < length - 1)
                        def _():
                            start(UP, other, piece)

                        @pl.when(line > 0)
                        def _():
                            start(DOWN, other, piece)

            for_each(0, PIECES, column)

            def crossed(piece, far=far):
                @pl.when(line >= far)
                def _():
                    arrive(other - 2 * far, piece)

                    @pl.when(line < length - 1)
                    def _():
                        start(UP, other - 2 * far, piece)

                @pl.when(line + far < length)
                def _():
                    arrive(other + 2 * far, piece)

                    @pl.when(line > 0)
                    def _():
                        start(DOWN, other + 2 * far, piece)

            for_each(0, CROSS_FIRST, crossed)
        for far in range(1, length):

            def last(piece, far=far):
                @pl.when(line >= far)
                def _():
                    arrive(other - 2 * far, piece)

                @pl.when(line + far < length)
                def _():
                    arrive(other + 2 * far, piece)

            for_each(CROSS_FIRST, PIECES, last)

    own.wait()
    relay((lambda way, source, piece: copy(way, source, piece).start(),
           lambda source, piece: copy(ACROSS, source, piece).wait_recv()))
    relay((lambda way, source, piece: copy(way, source, piece).wait_send(),
           lambda source, piece: None))


def gather_blocks(held, shards):
    return pl.pallas_call(
        functools.partial(gather_kernel, shards),
        name="gather_blocks",
        out_shape=jax.ShapeDtypeStruct((shards,) + held.shape, held.dtype),
        in_specs=[pl.BlockSpec(memory_space=pl.ANY)],
        out_specs=pl.BlockSpec(memory_space=pl.ANY),
        scratch_shapes=[
            pltpu.SemaphoreType.DMA((3, shards, PIECES)),
            pltpu.SemaphoreType.DMA((shards, PIECES)),
            pltpu.SemaphoreType.DMA,
        ],
        compiler_params=pltpu.CompilerParams(collective_id=0, has_side_effects=True),
    )(held)


def reduce_kernel(shards, grads_ref, out_ref, acc, below, above, across,
                  send_sem, below_sem, above_sem, across_sem, load_sem):
    me, line, side, length = neighbours(shards)
    size = out_ref.shape[0] // PIECES
    load = pltpu.make_async_copy(grads_ref, acc, load_sem)
    load.start()
    other = greet(me, line, length)
    load.wait()

    def part(piece):
        return pl.ds(piece * size, size)

    def copy(way, dest, piece):
        landing, sem, to = (
            (below, below_sem, me + 2),
            (above, above_sem, me - 2),
            (across, across_sem, other),
        )[way]
        return pltpu.make_async_remote_copy(
            src_ref=acc.at[dest, part(piece)], dst_ref=landing.at[dest, part(piece)],
            send_sem=send_sem.at[dest, piece], recv_sem=sem.at[dest, piece],
            device_id={"shard": to}, device_id_type=pl.DeviceIdType.MESH,
        )

    def for_each(first, last, body):
        def step(piece, carry):
            body(piece)
            return carry

        lax.fori_loop(first, last, step, 0)

    def add(way, dest, piece):
        copy(way, dest, piece).wait_recv()
        landing = (below, above, across)[way]
        total = (acc[dest, part(piece)].astype(jnp.float32)
                 + landing[dest, part(piece)].astype(jnp.float32))
        acc[dest, part(piece)] = total.astype(acc.dtype)

    def schedule(start, add):
        for far in range(length - 1, -1, -1):

            def cross(piece, far=far):
                @pl.when(line + far < length)
                def _():
                    start(ACROSS, other + 2 * far, piece)

                if far > 0:
                    @pl.when(line >= far)
                    def _():
                        start(ACROSS, other - 2 * far, piece)

            for_each(CROSS_FIRST, PIECES, cross)
        for far in range(length - 1, 0, -1):

            def along(piece, column, far=far):
                @pl.when(line + far < length)
                def _():
                    dest = column + 2 * far

                    @pl.when(piece >= CROSS_FIRST)
                    def _():
                        add(ACROSS, dest, piece)

                    @pl.when(line > 0)
                    def _():
                        add(UP, dest, piece)

                    start(UP, dest, piece)

                @pl.when(line >= far)
                def _():
                    dest = column - 2 * far

                    @pl.when(piece >= CROSS_FIRST)
                    def _():
                        add(ACROSS, dest, piece)

                    @pl.when(line < length - 1)
                    def _():
                        add(DOWN, dest, piece)

                    start(DOWN, dest, piece)

            def both(piece):
                along(piece, other)
                along(piece, me)

            for_each(0, CROSS_FIRST, both)
            for_each(CROSS_FIRST, PIECES, functools.partial(along, column=me))

        def turn(piece):
            @pl.when(line > 0)
            def _():
                add(UP, other, piece)

            @pl.when(line < length - 1)
            def _():
                add(DOWN, other, piece)

            start(ACROSS, other, piece)

        for_each(0, CROSS_FIRST, turn)

    schedule(lambda way, dest, piece: copy(way, dest, piece).start(), add)

    def finish(piece):
        @pl.when(line > 0)
        def _():
            add(UP, me, piece)

        @pl.when(line < length - 1)
        def _():
            add(DOWN, me, piece)

        add(ACROSS, me, piece)
        out_ref[part(piece)] = acc[me, part(piece)]

    for_each(CROSS_FIRST, PIECES, finish)
    for_each(0, CROSS_FIRST, finish)
    schedule(lambda way, dest, piece: copy(way, dest, piece).wait_send(),
             lambda way, dest, piece: None)


def reduce_blocks(grads, shards):
    shape = grads.shape
    sems = pltpu.SemaphoreType.DMA((shards, PIECES))
    buffer = pltpu.VMEM(shape, grads.dtype)
    return pl.pallas_call(
        functools.partial(reduce_kernel, shards),
        name="reduce_blocks",
        out_shape=jax.ShapeDtypeStruct(shape[1:], grads.dtype),
        in_specs=[pl.BlockSpec(memory_space=pl.ANY)],
        out_specs=pl.BlockSpec(memory_space=pltpu.VMEM),
        scratch_shapes=[buffer, buffer, buffer, buffer, sems, sems, sems, sems,
                        pltpu.SemaphoreType.DMA],
        compiler_params=pltpu.CompilerParams(
            collective_id=1, has_side_effects=True, vmem_limit_bytes=56 * MIB),
    )(grads)


def exchange(send):
    return lax.all_to_all(send, "shard", 0, 0, tiled=True)


def local(tokens, weight_slots, block_rows, block_owner, block_slot, grad_act):
    replicas = lax.axis_size("replica")
    shards = lax.axis_size("shard")
    replica = lax.axis_index("replica")
    me = lax.axis_index("shard")
    block = weight_slots.shape[3]
    cap = weight_slots.shape[1]
    tok_rows, width = tokens.shape[1], tokens.shape[2]
    keep = block_rows.shape[1]
    slice_cols = grad_act.shape[2] // block
    all_rows = replicas * tok_rows
    count = slice_cols * keep
    per_pair = -(-cap // shards)
    per_dev = -(-count // (shards * PIECES)) * PIECES
    own_slots = weight_slots.reshape(cap, block, block)

    start_col = replica * slice_cols
    rows = lax.dynamic_slice_in_dim(block_rows, start_col, slice_cols, 0).reshape(-1)
    place = (lax.dynamic_slice_in_dim(block_owner, start_col, slice_cols, 0) * cap
             + lax.dynamic_slice_in_dim(block_slot, start_col, slice_cols, 0)).reshape(-1)
    rank = jnp.sum((place[None, :] < place[:, None]).astype(jnp.int32), axis=1)
    where_at = (rank % shards) * per_dev + rank // shards
    ranks = jnp.arange(count, dtype=jnp.int32)
    by_rank = jnp.sum(jnp.where(rank[None, :] == ranks[:, None], place[None, :], 0), axis=1)
    owners = jnp.arange(shards, dtype=jnp.int32)
    first = jnp.sum((place[None, :] < owners[:, None] * cap).astype(jnp.int32), axis=1)

    turn = jnp.arange(per_pair, dtype=jnp.int32)[None, :]
    my_first = first[me]
    send_rank = my_first + (owners[:, None] - my_first) % shards + turn * shards
    send_slot = jnp.clip(jnp.take(by_rank, jnp.clip(send_rank, 0, count - 1)) - me * cap, 0, cap - 1)
    hold_rank = jnp.clip(jnp.arange(per_dev, dtype=jnp.int32) * shards + me, 0, count - 1)
    hold_owner = jnp.take(by_rank, hold_rank) // cap
    hold_first = jnp.take(first, hold_owner)
    hold_from = hold_owner * per_pair + (hold_rank - hold_first) // shards
    back_rank = first[:, None] + (me - first[:, None]) % shards + turn * shards
    back_from = jnp.clip((back_rank - me) // shards, 0, per_dev - 1)
    slots = me * cap + jnp.arange(cap, dtype=jnp.int32)
    slot_rank = jnp.sum((place[None, :] < slots[:, None]).astype(jnp.int32), axis=1)
    slot_used = jnp.any(place[None, :] == slots[:, None], axis=1)
    slot_from = jnp.clip((slot_rank % shards) * per_pair + (slot_rank - my_first) // shards,
                         0, shards * per_pair - 1)

    gathered = lax.all_gather(tokens, "replica", axis=0, tiled=True).reshape(all_rows, width)
    sent = jnp.take(own_slots, send_slot.reshape(-1), axis=0)
    got = exchange(sent)
    held = jnp.take(got, hold_from, axis=0)
    slab = gather_blocks(held, shards).reshape(shards * per_dev, block, block)
    tok_t = gathered.T

    cols = GROUP * block
    act_out, slope, grads = pl.pallas_call(
        functools.partial(forward_kernel, keep),
        name="forward_and_weight_grad",
        out_shape=(
            jax.ShapeDtypeStruct((replicas, tok_rows, slice_cols * block), jnp.bfloat16),
            jax.ShapeDtypeStruct((all_rows, slice_cols * block), jnp.bfloat16),
            jax.ShapeDtypeStruct((shards * per_dev, block, block), jnp.bfloat16),
        ),
        grid_spec=pltpu.PrefetchScalarGridSpec(
            num_scalar_prefetch=3,
            grid=(slice_cols // GROUP,),
            in_specs=[
                pl.BlockSpec((all_rows, width), lambda i, *_: (0, 0)),
                pl.BlockSpec((width, all_rows), lambda i, *_: (0, 0)),
                pl.BlockSpec((replicas, tok_rows, cols), lambda i, *_: (0, 0, i)),
                pl.BlockSpec(memory_space=pl.ANY),
            ],
            out_specs=(
                pl.BlockSpec((replicas, tok_rows, cols), lambda i, *_: (0, 0, i)),
                pl.BlockSpec((all_rows, cols), lambda i, *_: (0, i)),
                pl.BlockSpec(memory_space=pl.ANY),
            ),
            scratch_shapes=[
                pltpu.VMEM((2, width, cols), jnp.bfloat16),
                pltpu.VMEM((2, width, cols), jnp.bfloat16),
                pltpu.SemaphoreType.DMA((2,)),
                pltpu.SemaphoreType.DMA((2,)),
            ],
        ),
        compiler_params=pltpu.CompilerParams(vmem_limit_bytes=56 * MIB),
        cost_estimate=pl.CostEstimate(
            flops=4 * all_rows * width * slice_cols * block, transcendentals=0,
            bytes_accessed=60 * MIB,
        ),
    )(where_at, rows, where_at, gathered, tok_t, grad_act, slab)

    partial_grad = pl.pallas_call(
        functools.partial(input_grad_kernel, keep),
        name="token_grad",
        out_shape=jax.ShapeDtypeStruct((all_rows, width), jnp.bfloat16),
        grid_spec=pltpu.PrefetchScalarGridSpec(
            num_scalar_prefetch=2,
            grid=(slice_cols // GROUP,),
            in_specs=[
                pl.BlockSpec((all_rows, cols), lambda i, *_: (0, i)),
                pl.BlockSpec(memory_space=pl.ANY),
            ],
            out_specs=pl.BlockSpec((all_rows, width), lambda i, *_: (0, 0)),
            scratch_shapes=[
                pltpu.VMEM((2, width, cols), jnp.bfloat16),
                pltpu.VMEM((all_rows, width), jnp.float32),
                pltpu.SemaphoreType.DMA((2,)),
            ],
        ),
        compiler_params=pltpu.CompilerParams(vmem_limit_bytes=56 * MIB),
        cost_estimate=pl.CostEstimate(
            flops=2 * all_rows * width * slice_cols * block, transcendentals=0,
            bytes_accessed=30 * MIB,
        ),
    )(where_at, rows, slope, slab)

    grad_tokens = lax.psum_scatter(
        partial_grad.reshape(replicas, tok_rows, width), "replica", scatter_dimension=0, tiled=True
    )
    summed = reduce_blocks(grads.reshape(shards, per_dev, block, block), shards)
    summed = summed.reshape(per_dev, block, block)
    returned = exchange(jnp.take(summed, back_from.reshape(-1), axis=0))
    grad_scale = 1.0 / math.sqrt(replicas * shards * tok_rows)
    mine = jnp.take(returned, slot_from, axis=0).astype(jnp.float32) * grad_scale
    grad_slots = jnp.where(slot_used[:, None, None], mine, 0.0).reshape(1, cap, block, block)
    return (act_out, grad_tokens, grad_slots)


def solution(mesh):
    return jax.shard_map(
        local,
        mesh=mesh,
        in_specs=(
            P("replica", "shard", None),
            P("replica", "shard", None, None),
            P(),
            P(),
            P(),
            P(None, "shard", "replica"),
        ),
        out_specs=(
            P(None, "shard", "replica"),
            P("replica", "shard", None),
            P("replica", "shard", None, None),
        ),
        check_vma=False,
    )
```

```python
import functools
import math

import jax
import jax.numpy as jnp
from jax import lax
from jax.experimental import pallas as pl
from jax.experimental.pallas import tpu as pltpu
from jax.sharding import PartitionSpec as P

GROUP = 4
PIECES = 6
SPLIT = 3
MIB = 1 << 20


def gelu_both(hidden):
    cdf = 0.5 * (1.0 + lax.erf(hidden * 0.7071067811865476))
    slope = cdf + hidden * jnp.exp(-0.5 * hidden * hidden) * 0.3989422804014327
    return hidden * cdf, slope


def load_columns(step, slot, keep, idx_ref, rows_ref, slab_ref, wbuf, wsem):
    block = slab_ref.shape[1]
    wbuf[slot] = jnp.zeros(wbuf.shape[1:], wbuf.dtype)
    for col in range(GROUP):

        def body(j, carry, col=col):
            at = (step * GROUP + col) * keep + j
            row = pl.multiple_of(rows_ref[at] * block, block)
            pltpu.make_async_copy(
                slab_ref.at[idx_ref[at]],
                wbuf.at[slot, pl.ds(row, block), pl.ds(col * block, block)],
                wsem.at[slot],
            ).start()
            return carry

        lax.fori_loop(0, keep, body, 0)


def wait_columns(slot, keep, block, wbuf, wsem):
    part = wbuf.at[slot, pl.ds(0, keep * block), :]
    pltpu.make_async_copy(part, part, wsem.at[slot]).wait()


def forward_kernel(keep, idx_ref, rows_ref, pos_ref, tok_ref, tokt_ref, cot_ref, slab_ref,
                   act_ref, slope_ref, grads_ref, wbuf, gbuf, wsem, gsem):
    step = pl.program_id(0)
    steps = pl.num_programs(0)
    slot = lax.rem(step, 2)
    block = slab_ref.shape[1]
    rows = tok_ref.shape[0]
    width = tok_ref.shape[1]
    load = functools.partial(load_columns, keep=keep, idx_ref=idx_ref, rows_ref=rows_ref,
                             slab_ref=slab_ref, wbuf=wbuf, wsem=wsem)

    @pl.when(step == 0)
    def _():
        load(step, 0)

    @pl.when(step + 1 < steps)
    def _():
        load(step + 1, 1 - slot)

    wait_columns(slot, keep, block, wbuf, wsem)
    per = cot_ref.shape[1]

    def fwd(r, carry):
        at = pl.ds(pl.multiple_of(r * per, per), per)
        hidden = jnp.dot(tok_ref[at, :], wbuf[slot], preferred_element_type=jnp.float32)
        act, slope = gelu_both(hidden)
        act_ref[r] = act.astype(act_ref.dtype)
        slope = cot_ref[r].astype(jnp.float32) * slope
        slope_ref[at, :] = slope.astype(slope_ref.dtype)
        return carry

    lax.fori_loop(0, cot_ref.shape[0], fwd, 0)

    def drain(which):
        part = gbuf.at[which, pl.ds(0, keep * block), :]
        pltpu.make_async_copy(part, part, gsem.at[which]).wait()

    @pl.when(step >= 2)
    def _():
        drain(slot)

    tile = 512

    def back(m, carry):
        at = pl.ds(pl.multiple_of(m * tile, tile), tile)
        gbuf[slot, at, :] = jnp.dot(
            tokt_ref[at, :], slope_ref[...], preferred_element_type=jnp.float32
        ).astype(gbuf.dtype)
        return carry

    lax.fori_loop(0, width // tile, back, 0)

    for col in range(GROUP):

        def put(j, carry, col=col):
            at = (step * GROUP + col) * keep + j
            row = pl.multiple_of(rows_ref[at] * block, block)
            pltpu.make_async_copy(
                gbuf.at[slot, pl.ds(row, block), pl.ds(col * block, block)],
                grads_ref.at[pos_ref[at]],
                gsem.at[slot],
            ).start()
            return carry

        lax.fori_loop(0, keep, put, 0)

    @pl.when(step == steps - 1)
    def _():
        drain(slot)

        @pl.when(steps > 1)
        def _():
            drain(1 - slot)


def input_grad_kernel(keep, idx_ref, rows_ref, slope_ref, slab_ref, out_ref, wbuf, total, wsem):
    step = pl.program_id(0)
    steps = pl.num_programs(0)
    slot = lax.rem(step, 2)
    block = slab_ref.shape[1]
    load = functools.partial(load_columns, keep=keep, idx_ref=idx_ref, rows_ref=rows_ref,
                             slab_ref=slab_ref, wbuf=wbuf, wsem=wsem)

    @pl.when(step == 0)
    def _():
        load(step, 0)
        total[...] = jnp.zeros_like(total)

    @pl.when(step + 1 < steps)
    def _():
        load(step + 1, 1 - slot)

    wait_columns(slot, keep, block, wbuf, wsem)
    tile = 512

    def body(n, carry):
        at = pl.ds(pl.multiple_of(n * tile, tile), tile)
        total[:, at] += lax.dot_general(
            slope_ref[...], wbuf[slot, at, :], (((1,), (1,)), ((), ())),
            preferred_element_type=jnp.float32,
        )
        return carry

    lax.fori_loop(0, total.shape[1] // tile, body, 0)

    @pl.when(step == steps - 1)
    def _():
        out_ref[...] = total[...].astype(out_ref.dtype)


def ring_index(position, shards):
    position = lax.rem(position + shards, shards)
    half = shards // 2
    side = position // half
    return 2 * (position + side * (shards - 1 - 2 * position)) + side


def ring_place(shards):
    me = lax.axis_index("shard")
    line, side = me // 2, lax.rem(me, 2)
    here = line + side * (shards - 1 - 2 * line)
    ways = (ring_index(here + 1, shards), ring_index(here - 1, shards))
    barrier = pltpu.get_barrier_semaphore()
    for to in ways:
        pl.semaphore_signal(barrier, inc=1, device_id={"shard": to},
                            device_id_type=pl.DeviceIdType.MESH)
    pl.semaphore_wait(barrier, 2)
    return me, here, ways


def for_each(first, last, body):
    def step(piece, carry):
        body(piece)
        return carry

    lax.fori_loop(first, last, step, 0)


NEXT, LAST = 0, 1
SIGN = (1, -1)


def hop_pieces(way, hop, shards):
    if hop < shards // 2:
        return (0, PIECES)
    if hop > shards // 2:
        return (0, 0)
    return ((0, SPLIT), (SPLIT, PIECES))[way]


def gather_kernel(shards, held_ref, slab_ref, send_sem, recv_sem, own_sem):
    size = held_ref.shape[0] // PIECES
    me, here, ways = ring_place(shards)
    own = pltpu.make_async_copy(held_ref, slab_ref.at[me], own_sem)
    own.start()
    own.wait()

    def copy(way, source, piece):
        at = pl.ds(piece * size, size)
        return pltpu.make_async_remote_copy(
            src_ref=slab_ref.at[source, at], dst_ref=slab_ref.at[source, at],
            send_sem=send_sem.at[way, source, piece], recv_sem=recv_sem.at[source, piece],
            device_id={"shard": ways[way]}, device_id_type=pl.DeviceIdType.MESH,
        )

    def source(way, hop):
        return ring_index(here - SIGN[way] * hop, shards)

    def own_piece(piece):
        for way in (NEXT, LAST):
            copy(way, me, piece).start()

    for_each(0, PIECES, own_piece)
    for hop in range(1, shards // 2 + 1):

        def relay(piece, hop=hop):
            for way in (NEXT, LAST):
                first, last = hop_pieces(way, hop, shards)

                @pl.when((piece >= first) & (piece < last))
                def _(way=way):
                    copy(way, source(way, hop), piece).wait_recv()

                first, last = hop_pieces(way, hop + 1, shards)
                if last > first:

                    @pl.when((piece >= first) & (piece < last))
                    def _(way=way):
                        copy(way, source(way, hop), piece).start()

        for_each(0, PIECES, relay)
    for hop in range(1, shards // 2 + 1):
        for way in (NEXT, LAST):
            for_each(*hop_pieces(way, hop, shards),
                     lambda piece, way=way, hop=hop:
                     copy(way, source(way, hop - 1), piece).wait_send())


def gather_blocks(held, shards):
    return pl.pallas_call(
        functools.partial(gather_kernel, shards),
        name="gather_blocks",
        out_shape=jax.ShapeDtypeStruct((shards,) + held.shape, held.dtype),
        in_specs=[pl.BlockSpec(memory_space=pl.ANY)],
        out_specs=pl.BlockSpec(memory_space=pl.ANY),
        scratch_shapes=[
            pltpu.SemaphoreType.DMA((2, shards, PIECES)),
            pltpu.SemaphoreType.DMA((shards, PIECES)),
            pltpu.SemaphoreType.DMA,
        ],
        compiler_params=pltpu.CompilerParams(collective_id=0, has_side_effects=True),
    )(held)


def reduce_kernel(shards, grads_ref, out_ref, acc, landing, send_sem, recv_sem, load_sem):
    size = out_ref.shape[0] // PIECES
    load = pltpu.make_async_copy(grads_ref, acc, load_sem)
    load.start()
    me, here, ways = ring_place(shards)
    load.wait()

    def part(piece):
        return pl.ds(piece * size, size)

    def copy(way, dest, piece):
        return pltpu.make_async_remote_copy(
            src_ref=acc.at[dest, part(piece)], dst_ref=landing.at[way, dest, part(piece)],
            send_sem=send_sem.at[dest, piece], recv_sem=recv_sem.at[way, dest, piece],
            device_id={"shard": ways[way]}, device_id_type=pl.DeviceIdType.MESH,
        )

    def dest_at(way, hop):
        return ring_index(here + SIGN[way] * hop, shards)

    def add(way, dest, piece):
        copy(way, dest, piece).wait_recv()
        total = (acc[dest, part(piece)].astype(jnp.float32)
                 + landing[way, dest, part(piece)].astype(jnp.float32))
        acc[dest, part(piece)] = total.astype(acc.dtype)

    for hop in range(shards // 2, 0, -1):

        def relay(piece, hop=hop):
            for way in (NEXT, LAST):
                dest = dest_at(way, hop)
                first, last = hop_pieces(way, hop + 1, shards)
                if last > first:

                    @pl.when((piece >= first) & (piece < last))
                    def _(way=way, dest=dest):
                        add(way, dest, piece)

                first, last = hop_pieces(way, hop, shards)

                @pl.when((piece >= first) & (piece < last))
                def _(way=way, dest=dest):
                    copy(way, dest, piece).start()

        for_each(0, PIECES, relay)

    def finish(piece):
        total = acc[me, part(piece)].astype(jnp.float32)
        for way in (NEXT, LAST):
            copy(way, me, piece).wait_recv()
            total = total + landing[way, me, part(piece)].astype(jnp.float32)
        out_ref[part(piece)] = total.astype(out_ref.dtype)

    for_each(0, PIECES, finish)
    for hop in range(shards // 2, 0, -1):
        for way in (NEXT, LAST):
            for_each(*hop_pieces(way, hop, shards),
                     lambda piece, way=way, hop=hop:
                     copy(way, dest_at(way, hop), piece).wait_send())


def reduce_blocks(grads, shards):
    shape = grads.shape
    return pl.pallas_call(
        functools.partial(reduce_kernel, shards),
        name="reduce_blocks",
        out_shape=jax.ShapeDtypeStruct(shape[1:], grads.dtype),
        in_specs=[pl.BlockSpec(memory_space=pl.ANY)],
        out_specs=pl.BlockSpec(memory_space=pltpu.VMEM),
        scratch_shapes=[
            pltpu.VMEM(shape, grads.dtype),
            pltpu.VMEM((2,) + shape, grads.dtype),
            pltpu.SemaphoreType.DMA((shards, PIECES)),
            pltpu.SemaphoreType.DMA((2, shards, PIECES)),
            pltpu.SemaphoreType.DMA,
        ],
        compiler_params=pltpu.CompilerParams(
            collective_id=1, has_side_effects=True, vmem_limit_bytes=56 * MIB),
    )(grads)


def exchange(send):
    return lax.all_to_all(send, "shard", 0, 0, tiled=True)


def local(tokens, weight_slots, block_rows, block_owner, block_slot, grad_act):
    replicas = lax.axis_size("replica")
    shards = lax.axis_size("shard")
    replica = lax.axis_index("replica")
    me = lax.axis_index("shard")
    block = weight_slots.shape[3]
    cap = weight_slots.shape[1]
    tok_rows, width = tokens.shape[1], tokens.shape[2]
    keep = block_rows.shape[1]
    slice_cols = grad_act.shape[2] // block
    all_rows = replicas * tok_rows
    count = slice_cols * keep
    per_pair = -(-cap // shards)
    per_dev = -(-count // (shards * PIECES)) * PIECES
    own_slots = weight_slots.reshape(cap, block, block)

    start_col = replica * slice_cols
    rows = lax.dynamic_slice_in_dim(block_rows, start_col, slice_cols, 0).reshape(-1)
    place = (lax.dynamic_slice_in_dim(block_owner, start_col, slice_cols, 0) * cap
             + lax.dynamic_slice_in_dim(block_slot, start_col, slice_cols, 0)).reshape(-1)
    rank = jnp.sum((place[None, :] < place[:, None]).astype(jnp.int32), axis=1)
    where_at = (rank % shards) * per_dev + rank // shards
    ranks = jnp.arange(count, dtype=jnp.int32)
    by_rank = jnp.sum(jnp.where(rank[None, :] == ranks[:, None], place[None, :], 0), axis=1)
    owners = jnp.arange(shards, dtype=jnp.int32)
    first = jnp.sum((place[None, :] < owners[:, None] * cap).astype(jnp.int32), axis=1)

    turn = jnp.arange(per_pair, dtype=jnp.int32)[None, :]
    my_first = first[me]
    send_rank = my_first + (owners[:, None] - my_first) % shards + turn * shards
    send_slot = jnp.clip(jnp.take(by_rank, jnp.clip(send_rank, 0, count - 1)) - me * cap, 0, cap - 1)
    hold_rank = jnp.clip(jnp.arange(per_dev, dtype=jnp.int32) * shards + me, 0, count - 1)
    hold_owner = jnp.take(by_rank, hold_rank) // cap
    hold_first = jnp.take(first, hold_owner)
    hold_from = hold_owner * per_pair + (hold_rank - hold_first) // shards
    back_rank = first[:, None] + (me - first[:, None]) % shards + turn * shards
    back_from = jnp.clip((back_rank - me) // shards, 0, per_dev - 1)
    slots = me * cap + jnp.arange(cap, dtype=jnp.int32)
    slot_rank = jnp.sum((place[None, :] < slots[:, None]).astype(jnp.int32), axis=1)
    slot_used = jnp.any(place[None, :] == slots[:, None], axis=1)
    slot_from = jnp.clip((slot_rank % shards) * per_pair + (slot_rank - my_first) // shards,
                         0, shards * per_pair - 1)

    gathered = lax.all_gather(tokens, "replica", axis=0, tiled=True).reshape(all_rows, width)
    sent = jnp.take(own_slots, send_slot.reshape(-1), axis=0)
    got = exchange(sent)
    held = jnp.take(got, hold_from, axis=0)
    slab = gather_blocks(held, shards).reshape(shards * per_dev, block, block)
    tok_t = gathered.T

    cols = GROUP * block
    act_out, slope, grads = pl.pallas_call(
        functools.partial(forward_kernel, keep),
        name="forward_and_weight_grad",
        out_shape=(
            jax.ShapeDtypeStruct((replicas, tok_rows, slice_cols * block), jnp.bfloat16),
            jax.ShapeDtypeStruct((all_rows, slice_cols * block), jnp.bfloat16),
            jax.ShapeDtypeStruct((shards * per_dev, block, block), jnp.bfloat16),
        ),
        grid_spec=pltpu.PrefetchScalarGridSpec(
            num_scalar_prefetch=3,
            grid=(slice_cols // GROUP,),
            in_specs=[
                pl.BlockSpec((all_rows, width), lambda i, *_: (0, 0)),
                pl.BlockSpec((width, all_rows), lambda i, *_: (0, 0)),
                pl.BlockSpec((replicas, tok_rows, cols), lambda i, *_: (0, 0, i)),
                pl.BlockSpec(memory_space=pl.ANY),
            ],
            out_specs=(
                pl.BlockSpec((replicas, tok_rows, cols), lambda i, *_: (0, 0, i)),
                pl.BlockSpec((all_rows, cols), lambda i, *_: (0, i)),
                pl.BlockSpec(memory_space=pl.ANY),
            ),
            scratch_shapes=[
                pltpu.VMEM((2, width, cols), jnp.bfloat16),
                pltpu.VMEM((2, width, cols), jnp.bfloat16),
                pltpu.SemaphoreType.DMA((2,)),
                pltpu.SemaphoreType.DMA((2,)),
            ],
        ),
        compiler_params=pltpu.CompilerParams(vmem_limit_bytes=56 * MIB),
        cost_estimate=pl.CostEstimate(
            flops=4 * all_rows * width * slice_cols * block, transcendentals=0,
            bytes_accessed=60 * MIB,
        ),
    )(where_at, rows, where_at, gathered, tok_t, grad_act, slab)

    partial_grad = pl.pallas_call(
        functools.partial(input_grad_kernel, keep),
        name="token_grad",
        out_shape=jax.ShapeDtypeStruct((all_rows, width), jnp.bfloat16),
        grid_spec=pltpu.PrefetchScalarGridSpec(
            num_scalar_prefetch=2,
            grid=(slice_cols // GROUP,),
            in_specs=[
                pl.BlockSpec((all_rows, cols), lambda i, *_: (0, i)),
                pl.BlockSpec(memory_space=pl.ANY),
            ],
            out_specs=pl.BlockSpec((all_rows, width), lambda i, *_: (0, 0)),
            scratch_shapes=[
                pltpu.VMEM((2, width, cols), jnp.bfloat16),
                pltpu.VMEM((all_rows, width), jnp.float32),
                pltpu.SemaphoreType.DMA((2,)),
            ],
        ),
        compiler_params=pltpu.CompilerParams(vmem_limit_bytes=56 * MIB),
        cost_estimate=pl.CostEstimate(
            flops=2 * all_rows * width * slice_cols * block, transcendentals=0,
            bytes_accessed=30 * MIB,
        ),
    )(where_at, rows, slope, slab)

    grad_tokens = lax.psum_scatter(
        partial_grad.reshape(replicas, tok_rows, width), "replica", scatter_dimension=0, tiled=True
    )
    summed = reduce_blocks(grads.reshape(shards, per_dev, block, block), shards)
    summed = summed.reshape(per_dev, block, block)
    returned = exchange(jnp.take(summed, back_from.reshape(-1), axis=0))
    grad_scale = 1.0 / math.sqrt(replicas * shards * tok_rows)
    mine = jnp.take(returned, slot_from, axis=0).astype(jnp.float32) * grad_scale
    grad_slots = jnp.where(slot_used[:, None, None], mine, 0.0).reshape(1, cap, block, block)
    return (act_out, grad_tokens, grad_slots)


def solution(mesh):
    return jax.shard_map(
        local,
        mesh=mesh,
        in_specs=(
            P("replica", "shard", None),
            P("replica", "shard", None, None),
            P(),
            P(),
            P(),
            P(None, "shard", "replica"),
        ),
        out_specs=(
            P(None, "shard", "replica"),
            P("replica", "shard", None),
            P("replica", "shard", None, None),
        ),
        check_vma=False,
    )
```

```python
import functools
import math

import jax
import jax.numpy as jnp
from jax import lax
from jax.experimental import pallas as pl
from jax.experimental.pallas import tpu as pltpu
from jax.sharding import PartitionSpec as P

GROUP = 4
PIECES = 6
SPLIT = 3
MIB = 1 << 20


def gelu_both(hidden):
    cdf = 0.5 * (1.0 + lax.erf(hidden * 0.7071067811865476))
    slope = cdf + hidden * jnp.exp(-0.5 * hidden * hidden) * 0.3989422804014327
    return hidden * cdf, slope


def load_columns(step, slot, keep, idx_ref, rows_ref, slab_ref, wbuf, wsem):
    block = slab_ref.shape[1]
    wbuf[slot] = jnp.zeros(wbuf.shape[1:], wbuf.dtype)
    for col in range(GROUP):

        def body(j, carry, col=col):
            at = (step * GROUP + col) * keep + j
            row = pl.multiple_of(rows_ref[at] * block, block)
            pltpu.make_async_copy(
                slab_ref.at[idx_ref[at]],
                wbuf.at[slot, pl.ds(row, block), pl.ds(col * block, block)],
                wsem.at[slot],
            ).start()
            return carry

        lax.fori_loop(0, keep, body, 0)


def wait_columns(slot, keep, block, wbuf, wsem):
    part = wbuf.at[slot, pl.ds(0, keep * block), :]
    pltpu.make_async_copy(part, part, wsem.at[slot]).wait()


def forward_kernel(keep, idx_ref, rows_ref, pos_ref, tok_ref, tokt_ref, cot_ref, slab_ref,
                   act_ref, slope_ref, grads_ref, wbuf, gbuf, wsem, gsem):
    step = pl.program_id(0)
    steps = pl.num_programs(0)
    slot = lax.rem(step, 2)
    block = slab_ref.shape[1]
    rows = tok_ref.shape[0]
    width = tok_ref.shape[1]
    load = functools.partial(load_columns, keep=keep, idx_ref=idx_ref, rows_ref=rows_ref,
                             slab_ref=slab_ref, wbuf=wbuf, wsem=wsem)

    @pl.when(step == 0)
    def _():
        load(step, 0)

    @pl.when(step + 1 < steps)
    def _():
        load(step + 1, 1 - slot)

    wait_columns(slot, keep, block, wbuf, wsem)
    per = cot_ref.shape[1]

    def fwd(r, carry):
        at = pl.ds(pl.multiple_of(r * per, per), per)
        hidden = jnp.dot(tok_ref[at, :], wbuf[slot], preferred_element_type=jnp.float32)
        act, slope = gelu_both(hidden)
        act_ref[r] = act.astype(act_ref.dtype)
        slope = cot_ref[r].astype(jnp.float32) * slope
        slope_ref[at, :] = slope.astype(slope_ref.dtype)
        return carry

    lax.fori_loop(0, cot_ref.shape[0], fwd, 0)

    def drain(which):
        part = gbuf.at[which, pl.ds(0, keep * block), :]
        pltpu.make_async_copy(part, part, gsem.at[which]).wait()

    @pl.when(step >= 2)
    def _():
        drain(slot)

    tile = 512

    def back(m, carry):
        at = pl.ds(pl.multiple_of(m * tile, tile), tile)
        gbuf[slot, at, :] = jnp.dot(
            tokt_ref[at, :], slope_ref[...], preferred_element_type=jnp.float32
        ).astype(gbuf.dtype)
        return carry

    lax.fori_loop(0, width // tile, back, 0)

    for col in range(GROUP):

        def put(j, carry, col=col):
            at = (step * GROUP + col) * keep + j
            row = pl.multiple_of(rows_ref[at] * block, block)
            pltpu.make_async_copy(
                gbuf.at[slot, pl.ds(row, block), pl.ds(col * block, block)],
                grads_ref.at[pos_ref[at]],
                gsem.at[slot],
            ).start()
            return carry

        lax.fori_loop(0, keep, put, 0)

    @pl.when(step == steps - 1)
    def _():
        drain(slot)

        @pl.when(steps > 1)
        def _():
            drain(1 - slot)


def input_grad_kernel(keep, idx_ref, rows_ref, slope_ref, slab_ref, out_ref, wbuf, total, wsem):
    step = pl.program_id(0)
    steps = pl.num_programs(0)
    slot = lax.rem(step, 2)
    block = slab_ref.shape[1]
    load = functools.partial(load_columns, keep=keep, idx_ref=idx_ref, rows_ref=rows_ref,
                             slab_ref=slab_ref, wbuf=wbuf, wsem=wsem)

    @pl.when(step == 0)
    def _():
        load(step, 0)
        total[...] = jnp.zeros_like(total)

    @pl.when(step + 1 < steps)
    def _():
        load(step + 1, 1 - slot)

    wait_columns(slot, keep, block, wbuf, wsem)
    tile = 512

    def body(n, carry):
        at = pl.ds(pl.multiple_of(n * tile, tile), tile)
        total[:, at] += lax.dot_general(
            slope_ref[...], wbuf[slot, at, :], (((1,), (1,)), ((), ())),
            preferred_element_type=jnp.float32,
        )
        return carry

    lax.fori_loop(0, total.shape[1] // tile, body, 0)

    @pl.when(step == steps - 1)
    def _():
        out_ref[...] = total[...].astype(out_ref.dtype)


def ring_index(position, shards):
    position = lax.rem(position + shards, shards)
    half = shards // 2
    side = position // half
    return 2 * (position + side * (shards - 1 - 2 * position)) + side


def ring_place(shards):
    me = lax.axis_index("shard")
    line, side = me // 2, lax.rem(me, 2)
    here = line + side * (shards - 1 - 2 * line)
    ways = (ring_index(here + 1, shards), ring_index(here - 1, shards))
    barrier = pltpu.get_barrier_semaphore()
    for to in ways:
        pl.semaphore_signal(barrier, inc=1, device_id={"shard": to},
                            device_id_type=pl.DeviceIdType.MESH)
    pl.semaphore_wait(barrier, 2)
    return me, here, ways


def for_each(first, last, body):
    def step(piece, carry):
        body(piece)
        return carry

    lax.fori_loop(first, last, step, 0)


NEXT, LAST = 0, 1
SIGN = (1, -1)


def hop_pieces(way, hop, shards):
    if hop < shards // 2:
        return (0, PIECES)
    if hop > shards // 2:
        return (0, 0)
    return ((0, SPLIT), (SPLIT, PIECES))[way]


def gather_kernel(shards, held_ref, out_ref, slab_ref, send_sem, recv_sem, out_sem, own_sem):
    size = held_ref.shape[0] // PIECES
    me, here, ways = ring_place(shards)
    own = pltpu.make_async_copy(held_ref, slab_ref.at[me], own_sem)
    own.start()
    own.wait()

    def copy(way, source, piece):
        at = pl.ds(piece * size, size)
        return pltpu.make_async_remote_copy(
            src_ref=slab_ref.at[source, at], dst_ref=slab_ref.at[source, at],
            send_sem=send_sem.at[way, source, piece], recv_sem=recv_sem.at[source, piece],
            device_id={"shard": ways[way]}, device_id_type=pl.DeviceIdType.MESH,
        )

    def store(source, piece):
        at = pl.ds(piece * size, size)
        return pltpu.make_async_copy(
            slab_ref.at[source, at], out_ref.at[source, at], out_sem.at[source, piece])

    def source(way, hop):
        return ring_index(here - SIGN[way] * hop, shards)

    def own_piece(piece):
        for way in (NEXT, LAST):
            copy(way, me, piece).start()
        store(me, piece).start()

    for_each(0, PIECES, own_piece)
    for hop in range(1, shards // 2 + 1):

        def relay(piece, hop=hop):
            for way in (NEXT, LAST):
                first, last = hop_pieces(way, hop, shards)

                @pl.when((piece >= first) & (piece < last))
                def _(way=way):
                    copy(way, source(way, hop), piece).wait_recv()

                first, last = hop_pieces(way, hop + 1, shards)
                if last > first:

                    @pl.when((piece >= first) & (piece < last))
                    def _(way=way):
                        copy(way, source(way, hop), piece).start()

                first, last = hop_pieces(way, hop, shards)

                @pl.when((piece >= first) & (piece < last))
                def _(way=way):
                    store(source(way, hop), piece).start()

        for_each(0, PIECES, relay)
    for_each(0, PIECES, lambda piece: store(me, piece).wait())
    for hop in range(1, shards // 2 + 1):
        for way in (NEXT, LAST):
            for_each(*hop_pieces(way, hop, shards),
                     lambda piece, way=way, hop=hop:
                     copy(way, source(way, hop - 1), piece).wait_send())
            for_each(*hop_pieces(way, hop, shards),
                     lambda piece, way=way, hop=hop:
                     store(source(way, hop), piece).wait())


def gather_blocks(held, shards):
    return pl.pallas_call(
        functools.partial(gather_kernel, shards),
        name="gather_blocks",
        out_shape=jax.ShapeDtypeStruct((shards,) + held.shape, held.dtype),
        in_specs=[pl.BlockSpec(memory_space=pl.ANY)],
        out_specs=pl.BlockSpec(memory_space=pl.ANY),
        scratch_shapes=[
            pltpu.VMEM((shards,) + held.shape, held.dtype),
            pltpu.SemaphoreType.DMA((2, shards, PIECES)),
            pltpu.SemaphoreType.DMA((shards, PIECES)),
            pltpu.SemaphoreType.DMA((shards, PIECES)),
            pltpu.SemaphoreType.DMA,
        ],
        compiler_params=pltpu.CompilerParams(
            collective_id=0, has_side_effects=True, vmem_limit_bytes=32 * MIB),
    )(held)


def reduce_kernel(shards, grads_ref, out_ref, acc, landing, send_sem, recv_sem, load_sem):
    size = out_ref.shape[0] // PIECES
    load = pltpu.make_async_copy(grads_ref, acc, load_sem)
    load.start()
    me, here, ways = ring_place(shards)
    load.wait()

    def part(piece):
        return pl.ds(piece * size, size)

    def copy(way, dest, piece):
        return pltpu.make_async_remote_copy(
            src_ref=acc.at[dest, part(piece)], dst_ref=landing.at[way, dest, part(piece)],
            send_sem=send_sem.at[dest, piece], recv_sem=recv_sem.at[way, dest, piece],
            device_id={"shard": ways[way]}, device_id_type=pl.DeviceIdType.MESH,
        )

    def dest_at(way, hop):
        return ring_index(here + SIGN[way] * hop, shards)

    def add(way, dest, piece):
        copy(way, dest, piece).wait_recv()
        total = (acc[dest, part(piece)].astype(jnp.float32)
                 + landing[way, dest, part(piece)].astype(jnp.float32))
        acc[dest, part(piece)] = total.astype(acc.dtype)

    for hop in range(shards // 2, 0, -1):

        def relay(piece, hop=hop):
            for way in (NEXT, LAST):
                dest = dest_at(way, hop)
                first, last = hop_pieces(way, hop + 1, shards)
                if last > first:

                    @pl.when((piece >= first) & (piece < last))
                    def _(way=way, dest=dest):
                        add(way, dest, piece)

                first, last = hop_pieces(way, hop, shards)

                @pl.when((piece >= first) & (piece < last))
                def _(way=way, dest=dest):
                    copy(way, dest, piece).start()

        for_each(0, PIECES, relay)

    def finish(piece):
        total = acc[me, part(piece)].astype(jnp.float32)
        for way in (NEXT, LAST):
            copy(way, me, piece).wait_recv()
            total = total + landing[way, me, part(piece)].astype(jnp.float32)
        out_ref[part(piece)] = total.astype(out_ref.dtype)

    for_each(0, PIECES, finish)
    for hop in range(shards // 2, 0, -1):
        for way in (NEXT, LAST):
            for_each(*hop_pieces(way, hop, shards),
                     lambda piece, way=way, hop=hop:
                     copy(way, dest_at(way, hop), piece).wait_send())


def reduce_blocks(grads, shards):
    shape = grads.shape
    return pl.pallas_call(
        functools.partial(reduce_kernel, shards),
        name="reduce_blocks",
        out_shape=jax.ShapeDtypeStruct(shape[1:], grads.dtype),
        in_specs=[pl.BlockSpec(memory_space=pl.ANY)],
        out_specs=pl.BlockSpec(memory_space=pltpu.VMEM),
        scratch_shapes=[
            pltpu.VMEM(shape, grads.dtype),
            pltpu.VMEM((2,) + shape, grads.dtype),
            pltpu.SemaphoreType.DMA((shards, PIECES)),
            pltpu.SemaphoreType.DMA((2, shards, PIECES)),
            pltpu.SemaphoreType.DMA,
        ],
        compiler_params=pltpu.CompilerParams(
            collective_id=1, has_side_effects=True, vmem_limit_bytes=56 * MIB),
    )(grads)


def exchange(send):
    return lax.all_to_all(send, "shard", 0, 0, tiled=True)


def local(tokens, weight_slots, block_rows, block_owner, block_slot, grad_act):
    replicas = lax.axis_size("replica")
    shards = lax.axis_size("shard")
    replica = lax.axis_index("replica")
    me = lax.axis_index("shard")
    block = weight_slots.shape[3]
    cap = weight_slots.shape[1]
    tok_rows, width = tokens.shape[1], tokens.shape[2]
    keep = block_rows.shape[1]
    slice_cols = grad_act.shape[2] // block
    all_rows = replicas * tok_rows
    count = slice_cols * keep
    per_pair = -(-cap // shards)
    per_dev = -(-count // (shards * PIECES)) * PIECES
    own_slots = weight_slots.reshape(cap, block, block)

    start_col = replica * slice_cols
    rows = lax.dynamic_slice_in_dim(block_rows, start_col, slice_cols, 0).reshape(-1)
    place = (lax.dynamic_slice_in_dim(block_owner, start_col, slice_cols, 0) * cap
             + lax.dynamic_slice_in_dim(block_slot, start_col, slice_cols, 0)).reshape(-1)
    rank = jnp.sum((place[None, :] < place[:, None]).astype(jnp.int32), axis=1)
    where_at = (rank % shards) * per_dev + rank // shards
    ranks = jnp.arange(count, dtype=jnp.int32)
    by_rank = jnp.sum(jnp.where(rank[None, :] == ranks[:, None], place[None, :], 0), axis=1)
    owners = jnp.arange(shards, dtype=jnp.int32)
    first = jnp.sum((place[None, :] < owners[:, None] * cap).astype(jnp.int32), axis=1)

    turn = jnp.arange(per_pair, dtype=jnp.int32)[None, :]
    my_first = first[me]
    send_rank = my_first + (owners[:, None] - my_first) % shards + turn * shards
    send_slot = jnp.clip(jnp.take(by_rank, jnp.clip(send_rank, 0, count - 1)) - me * cap, 0, cap - 1)
    hold_rank = jnp.clip(jnp.arange(per_dev, dtype=jnp.int32) * shards + me, 0, count - 1)
    hold_owner = jnp.take(by_rank, hold_rank) // cap
    hold_first = jnp.take(first, hold_owner)
    hold_from = hold_owner * per_pair + (hold_rank - hold_first) // shards
    back_rank = first[:, None] + (me - first[:, None]) % shards + turn * shards
    back_from = jnp.clip((back_rank - me) // shards, 0, per_dev - 1)
    slots = me * cap + jnp.arange(cap, dtype=jnp.int32)
    slot_rank = jnp.sum((place[None, :] < slots[:, None]).astype(jnp.int32), axis=1)
    slot_used = jnp.any(place[None, :] == slots[:, None], axis=1)
    slot_from = jnp.clip((slot_rank % shards) * per_pair + (slot_rank - my_first) // shards,
                         0, shards * per_pair - 1)

    gathered = lax.all_gather(tokens, "replica", axis=0, tiled=True).reshape(all_rows, width)
    sent = jnp.take(own_slots, send_slot.reshape(-1), axis=0)
    got = exchange(sent)
    held = jnp.take(got, hold_from, axis=0)
    slab = gather_blocks(held, shards).reshape(shards * per_dev, block, block)
    tok_t = gathered.T

    cols = GROUP * block
    act_out, slope, grads = pl.pallas_call(
        functools.partial(forward_kernel, keep),
        name="forward_and_weight_grad",
        out_shape=(
            jax.ShapeDtypeStruct((replicas, tok_rows, slice_cols * block), jnp.bfloat16),
            jax.ShapeDtypeStruct((all_rows, slice_cols * block), jnp.bfloat16),
            jax.ShapeDtypeStruct((shards * per_dev, block, block), jnp.bfloat16),
        ),
        grid_spec=pltpu.PrefetchScalarGridSpec(
            num_scalar_prefetch=3,
            grid=(slice_cols // GROUP,),
            in_specs=[
                pl.BlockSpec((all_rows, width), lambda i, *_: (0, 0)),
                pl.BlockSpec((width, all_rows), lambda i, *_: (0, 0)),
                pl.BlockSpec((replicas, tok_rows, cols), lambda i, *_: (0, 0, i)),
                pl.BlockSpec(memory_space=pl.ANY),
            ],
            out_specs=(
                pl.BlockSpec((replicas, tok_rows, cols), lambda i, *_: (0, 0, i)),
                pl.BlockSpec((all_rows, cols), lambda i, *_: (0, i)),
                pl.BlockSpec(memory_space=pl.ANY),
            ),
            scratch_shapes=[
                pltpu.VMEM((2, width, cols), jnp.bfloat16),
                pltpu.VMEM((2, width, cols), jnp.bfloat16),
                pltpu.SemaphoreType.DMA((2,)),
                pltpu.SemaphoreType.DMA((2,)),
            ],
        ),
        compiler_params=pltpu.CompilerParams(vmem_limit_bytes=56 * MIB),
        cost_estimate=pl.CostEstimate(
            flops=4 * all_rows * width * slice_cols * block, transcendentals=0,
            bytes_accessed=60 * MIB,
        ),
    )(where_at, rows, where_at, gathered, tok_t, grad_act, slab)

    partial_grad = pl.pallas_call(
        functools.partial(input_grad_kernel, keep),
        name="token_grad",
        out_shape=jax.ShapeDtypeStruct((all_rows, width), jnp.bfloat16),
        grid_spec=pltpu.PrefetchScalarGridSpec(
            num_scalar_prefetch=2,
            grid=(slice_cols // GROUP,),
            in_specs=[
                pl.BlockSpec((all_rows, cols), lambda i, *_: (0, i)),
                pl.BlockSpec(memory_space=pl.ANY),
            ],
            out_specs=pl.BlockSpec((all_rows, width), lambda i, *_: (0, 0)),
            scratch_shapes=[
                pltpu.VMEM((2, width, cols), jnp.bfloat16),
                pltpu.VMEM((all_rows, width), jnp.float32),
                pltpu.SemaphoreType.DMA((2,)),
            ],
        ),
        compiler_params=pltpu.CompilerParams(vmem_limit_bytes=56 * MIB),
        cost_estimate=pl.CostEstimate(
            flops=2 * all_rows * width * slice_cols * block, transcendentals=0,
            bytes_accessed=30 * MIB,
        ),
    )(where_at, rows, slope, slab)

    grad_tokens = lax.psum_scatter(
        partial_grad.reshape(replicas, tok_rows, width), "replica", scatter_dimension=0, tiled=True
    )
    summed = reduce_blocks(grads.reshape(shards, per_dev, block, block), shards)
    summed = summed.reshape(per_dev, block, block)
    returned = exchange(jnp.take(summed, back_from.reshape(-1), axis=0))
    grad_scale = 1.0 / math.sqrt(replicas * shards * tok_rows)
    mine = jnp.take(returned, slot_from, axis=0).astype(jnp.float32) * grad_scale
    grad_slots = jnp.where(slot_used[:, None, None], mine, 0.0).reshape(1, cap, block, block)
    return (act_out, grad_tokens, grad_slots)


def solution(mesh):
    return jax.shard_map(
        local,
        mesh=mesh,
        in_specs=(
            P("replica", "shard", None),
            P("replica", "shard", None, None),
            P(),
            P(),
            P(),
            P(None, "shard", "replica"),
        ),
        out_specs=(
            P(None, "shard", "replica"),
            P("replica", "shard", None),
            P("replica", "shard", None, None),
        ),
        check_vma=False,
    )
```
